32 devices in a mesh: groups: 2 (over y), wide: 8 (over z, x), narrow: 2 (over core).
Axes of the slice: x: 2, y: 2, z: 4, core: 2. Of those that a mesh axis runs over, the one named last changes fastest.
Arguments:
- queries: bfloat16 [4, 2048, 64], P(('groups', 'narrow'), 'wide'), parts along dimension 0, may hold values from -6 to 6
- key_rows: bfloat16 [4, 2048, 64], P(('groups', 'narrow'), 'wide'), parts along dimension 0, may hold values from -6 to 6
- values: bfloat16 [4, 2048, 64], P(('groups', 'narrow'), 'wide'), parts along dimension 0, may hold values from -6 to 6
- log_gate: float32 [4, 2048], P(('groups', 'narrow'), 'wide'), parts along dimension 0, may hold values from -0.8 to 0, as said below
- lengths: int32 [4], P(('groups', 'narrow')), parts along dimension 0, may hold values from 1024 to 2048
- cont_queries: bfloat16 [160, 64], P(('groups', 'wide', 'narrow')), parts along dimension 0, may hold values from -6 to 6
- cont_prompt: int32 [160], P(('groups', 'wide', 'narrow')), parts along dimension 0, may hold values from 0 to 1
Outputs:
- prompt_out: bfloat16 [4, 2048, 64], P(('groups', 'narrow'), 'wide'), parts along dimension 0
- cont_out: bfloat16 [160, 64], P(('groups', 'wide', 'narrow')), parts along dimension 0
The draws below stay inside these ranges and needn't reach their ends.
There are 2 independent parts, one for each index of `groups`. The reference program is written for one: setup_inputs(seed, part) draws one part's arguments, and reference() takes and returns one part's arrays. A program takes and returns all parts, laid end to end along the dimension named above; each array names one. Nothing has to cross between parts.
Inputs may be any that keep to these rules, and one draw needn't show every extreme that they name: `log_gate`: gates only shrink the state: every entry is at most zero.
All inputs are finite; a program needn't handle non-finite values.
Results may differ from the reference program's by a relative error of at most 0.0067.
Values may be sent and summed in bfloat16 or wider, within the bound.
A program may use at most 64 MiB of HBM per device.

```python
import jax
import jax.numpy as jnp
from jax import lax

D = 64
TOK = 256
PROMPTS = 2
SEQ = 2048
CONT = 80
N_WIDE = 8


def draw_log_gate(key, part):
    streams = jax.random.split(jax.random.fold_in(key, 11), 6)
    slow_rate = jax.random.uniform(streams[0], (PROMPTS,), jnp.float32, 0.2, 0.6) / SEQ
    fast_rate = 1.0 / jnp.exp(jax.random.uniform(streams[1], (PROMPTS,), jnp.float32, jnp.log(30.0), jnp.log(50.0)))
    chosen = jax.random.randint(streams[2], (), 0, PROMPTS)
    forget_speed = jnp.where(jnp.arange(PROMPTS) == chosen, fast_rate, slow_rate)
    forget_multiplier = jnp.exp(jax.random.uniform(streams[3], (PROMPTS, SEQ), jnp.float32, jnp.log(0.5), jnp.log(2.0)))
    spots = jax.random.randint(streams[4], (PROMPTS, 2), 0, SEQ)
    deviation_sums = jax.random.uniform(streams[5], (PROMPTS, 2), jnp.float32, 0.2, 0.5)
    agreeing_number = jnp.arange(SEQ)[None, :, None] == spots[:, None, :]
    span_extent = jnp.sum(jnp.where(agreeing_number, jnp.log(1.0 - deviation_sums)[:, None, :], 0.0), axis=2)
    return (-forget_speed[:, None] * forget_multiplier + span_extent).astype(jnp.float32)


def touch_ends(entries, rng, low, top_value):
    shape = entries.shape
    place = [jax.random.randint(jax.random.fold_in(rng, axis), (), 0, shape[axis]) for axis in range(len(shape))]
    entries = entries.at[tuple(place)].set(low)
    longest = shape.index(max(shape))
    place[longest] = (place[longest] + 1) % shape[longest]
    return entries.at[tuple(place)].set(top_value)


def block_levels(stream_key, extent, shards, least, largest):
    level, own = 1.0, jax.random.fold_in(stream_key, 6)
    for dim, parts in shards:
        steps = jnp.exp(jax.random.uniform(jax.random.fold_in(own, dim), (parts,), jnp.float32, least / len(shards), largest / len(shards)))
        level = level * jnp.repeat(steps, extent[dim] // parts).reshape([-1 if axis == dim else 1 for axis in range(len(extent))])
    return level


def gaussian(stream_key, shape, scale, limit, cuts=(), held_as=jnp.bfloat16):
    entries = scale * jax.random.normal(stream_key, shape, jnp.float32)
    if cuts:
        entries = entries * block_levels(stream_key, shape, cuts, -0.22, 0.18)
    return jnp.clip(entries, -limit, limit).astype(held_as)


def setup_inputs(seed: int = 0, part: int = 0) -> dict:
    key_list = jax.random.split(jax.random.key(seed), 8)
    part_splits = jax.random.split(jax.random.fold_in(key_list[7], part), 8)
    return {
        "queries": gaussian(part_splits[0], (PROMPTS, SEQ, D), 1.0, 6.0, ((0, 2), (1, 8))),
        "key_rows": gaussian(part_splits[1], (PROMPTS, SEQ, D), 1.0, 6.0, ((0, 2), (1, 8))),
        "values": gaussian(part_splits[2], (PROMPTS, SEQ, D), 1.0, 6.0, ((0, 2), (1, 8))),
        "log_gate": draw_log_gate(jax.random.fold_in(jax.random.fold_in(key_list[7], part), 71), part),
        "lengths": jax.random.randint(part_splits[4], (PROMPTS,), SEQ // 2, SEQ + 1).astype(jnp.int32),
        "cont_queries": gaussian(part_splits[5], (CONT, D), 1.0, 6.0, ((0, 16),)),
        "cont_prompt": touch_ends(jax.random.randint(part_splits[6], (CONT,), 0, PROMPTS), jax.random.fold_in(part_splits[6], 1), 0, PROMPTS - 1).astype(jnp.int32),
    }


epsilon = 1e-06

def rms_rows(running):
    return running * lax.rsqrt(lax.optimization_barrier(jnp.mean(running * running, axis=-1, keepdims=True)) + epsilon)

def pair_features(rows):
    wide_rows = rows.astype(jnp.float32)
    outer = wide_rows[:, :, None] * wide_rows[:, None, :]
    return outer.reshape(rows.shape[0], rows.shape[1] * rows.shape[1]).astype(jnp.bfloat16)

def shard_pass(query_rows, key_rows, payload_lines, gate_log, live_mask, carried):
    row_count, head_width = key_rows.shape
    gate_live = gate_log * live_mask
    cumulative = jnp.cumsum(gate_live)
    scores = lax.dot_general(query_rows, key_rows, (((1,), (1,)), ((), ())), preferred_element_type=jnp.float32)
    row_ids = jnp.arange(row_count, dtype=jnp.int32)
    lower_mask = row_ids[:, None] >= row_ids[None, :]
    decay_matrix = jnp.exp(jnp.where(lower_mask, cumulative[:, None] - cumulative[None, :], -jnp.inf))
    weights = (scores * scores * decay_matrix * live_mask[None, :]).astype(jnp.bfloat16)
    local_term = jnp.dot(weights, payload_lines, preferred_element_type=jnp.float32)
    carried_term = jnp.dot(pair_features(query_rows), carried, preferred_element_type=jnp.float32)
    running = local_term + jnp.exp(cumulative)[:, None] * carried_term
    output = (live_mask[:, None] * rms_rows(running)).astype(jnp.bfloat16)
    piece_number = cumulative[-1]
    scaled = live_mask * jnp.exp(piece_number - cumulative)
    spread = (scaled[:, None] * payload_lines.astype(jnp.float32)).astype(jnp.bfloat16)
    span_state = lax.dot_general(pair_features(key_rows), spread, (((0,), (0,)), ((), ())), preferred_element_type=jnp.float32)
    return (output, span_state.astype(jnp.bfloat16), piece_number)

def prompt_pass(query_everything, key_all, value_all, gate_all, length):
    position = jnp.arange(SEQ, dtype=jnp.int32)
    live_all = (position < length).astype(jnp.float32)

    def shard_step(carry, shard_item):
        query_rows, key_rows, payload_lines, gate_log, live_mask = shard_item
        output, span_state, piece_number = shard_pass(query_rows, key_rows, payload_lines, gate_log, live_mask, carry.astype(jnp.bfloat16))
        carry = jnp.exp(piece_number) * carry + span_state.astype(jnp.float32)
        return (carry, output)
    shard_items = (query_everything.reshape(N_WIDE, TOK, D), key_all.reshape(N_WIDE, TOK, D), value_all.reshape(N_WIDE, TOK, D), gate_all.reshape(N_WIDE, TOK), live_all.reshape(N_WIDE, TOK))
    initial = jnp.zeros((D * D, D), jnp.float32)
    final_state, outputs = lax.scan(shard_step, initial, shard_items)
    return (outputs.reshape(SEQ, D), final_state.astype(jnp.bfloat16))

def reference(queries, key_rows, values, log_gate, lengths, cont_queries, cont_prompt):
    outputs = []
    running = jnp.zeros((CONT, D), jnp.float32)
    cont_pairs = pair_features(cont_queries)
    for prompt_index in range(PROMPTS):
        output, final_state = prompt_pass(queries[prompt_index], key_rows[prompt_index], values[prompt_index], log_gate[prompt_index], lengths[prompt_index])
        outputs.append(output)
        partial_value = jnp.dot(cont_pairs, final_state, preferred_element_type=jnp.float32)
        running = jnp.where((cont_prompt == prompt_index)[:, None], partial_value, running)
    return (jnp.stack(outputs), rms_rows(running).astype(jnp.bfloat16))
```

```python
import functools

import jax
import jax.numpy as jnp
import numpy as np
from jax import lax
from jax.experimental import pallas as pl
from jax.experimental.pallas import tpu as pltpu
from jax.sharding import PartitionSpec as P

epsilon = 1e-06
block_rows = 1024


def rms_rows(running):
    return running * lax.rsqrt(jnp.mean(running * running, axis=-1, keepdims=True) + epsilon)


def extend_zeros(table, pad_count):
    return np.concatenate([table, np.zeros((pad_count,), table.dtype)])


def pair_tables(head_width, shard_count):
    lead_index, trail_index = np.triu_indices(head_width)
    doubled = np.where(lead_index == trail_index, 1.0, 2.0)
    feature_count = lead_index.shape[0]
    padded_rows = -(-feature_count // shard_count) * shard_count
    block_width = min(block_rows, padded_rows)
    full_length = -(-padded_rows // block_width) * block_width
    pad_count = full_length - lead_index.shape[0]
    lead_index = extend_zeros(lead_index, pad_count).astype(np.int32)
    trail_index = extend_zeros(trail_index, pad_count).astype(np.int32)
    doubled = extend_zeros(doubled, pad_count).astype(np.float32)
    live_pairs = (doubled > 0).astype(np.float32)
    return (
        jnp.asarray(lead_index),
        jnp.asarray(trail_index),
        jnp.asarray(doubled),
        jnp.asarray(live_pairs),
        padded_rows,
        block_width,
        full_length,
    )


def pair_block(rows, lead_part, trail_part, forget_multiplier):
    leading_columns = jnp.take(rows, lead_part, axis=1).astype(jnp.float32)
    right_cols = jnp.take(rows, trail_part, axis=1).astype(jnp.float32)
    return (leading_columns * right_cols * forget_multiplier[None, :]).astype(jnp.bfloat16)


def block_state(key_rows, spread, tables):
    lead_all, trail_all, doubled_all, live_pairs, padded_rows, block_width, full_length = tables
    head_width = key_rows.shape[1]

    def fill_block(block_index, state):
        first_row = block_index * block_width
        features = pair_block(
            key_rows,
            lax.dynamic_slice_in_dim(lead_all, first_row, block_width),
            lax.dynamic_slice_in_dim(trail_all, first_row, block_width),
            lax.dynamic_slice_in_dim(live_pairs, first_row, block_width),
        )
        state_block = lax.dot_general(
            features, spread, (((0,), (0,)), ((), ())), preferred_element_type=jnp.float32
        )
        return lax.dynamic_update_slice_in_dim(
            state, state_block.astype(jnp.bfloat16), first_row, 0
        )

    initial = jnp.zeros((full_length, head_width), jnp.bfloat16)
    return lax.fori_loop(0, full_length // block_width, fill_block, initial)[:padded_rows]


def carried_read(query_rows, carried, tables):
    lead_all, trail_all, doubled_all, live_pairs, padded_rows, block_width, full_length = tables
    row_count, head_width = query_rows.shape
    if full_length > padded_rows:
        carried = jnp.pad(carried, ((0, full_length - padded_rows), (0, 0)))

    def add_block(block_index, running):
        first_row = block_index * block_width
        features = pair_block(
            query_rows,
            lax.dynamic_slice_in_dim(lead_all, first_row, block_width),
            lax.dynamic_slice_in_dim(trail_all, first_row, block_width),
            lax.dynamic_slice_in_dim(doubled_all, first_row, block_width),
        )
        state_rows = lax.dynamic_slice_in_dim(carried, first_row, block_width, 0)
        return running + jnp.dot(features, state_rows, preferred_element_type=jnp.float32)

    return lax.fori_loop(
        0, full_length // block_width, add_block, jnp.zeros((row_count, head_width), jnp.float32)
    )


def owner_prefix(sent_slices, totals):
    shard_count = totals.shape[0]
    inclusive = jnp.cumsum(totals)
    exclusive = jnp.concatenate([jnp.zeros((1,), jnp.float32), inclusive])
    target = lax.iota(jnp.int32, shard_count + 1)[:, None]
    source = lax.iota(jnp.int32, shard_count)[None, :]
    weight = jnp.exp(jnp.where(source < target, exclusive[:, None] - inclusive[None, :], -jnp.inf))
    return jnp.einsum(
        "wu,urn->wrn", weight, sent_slices.astype(jnp.float32), precision=lax.Precision.HIGHEST
    )


def prompt_rows(query_rows, key_rows, payload_lines, cumulative, live_mask, carried, tables):
    row_count, head_width = query_rows.shape
    scores = lax.dot_general(
        query_rows, key_rows, (((1,), (1,)), ((), ())), preferred_element_type=jnp.float32
    )
    row_ids = lax.iota(jnp.int32, row_count)
    lower_mask = row_ids[:, None] >= row_ids[None, :]
    decay_matrix = jnp.exp(
        jnp.where(lower_mask, cumulative[:, None] - cumulative[None, :], -jnp.inf)
    )
    weights = (scores * scores * decay_matrix * live_mask[None, :]).astype(jnp.bfloat16)
    local_term = jnp.dot(weights, payload_lines, preferred_element_type=jnp.float32)
    carried_term = carried_read(query_rows, carried, tables)
    running = local_term + jnp.exp(cumulative)[:, None] * carried_term
    return (live_mask[:, None] * rms_rows(running)).astype(jnp.bfloat16)


def on_device(queries, key_rows, values, log_gate, lengths, cont_queries, cont_prompt):
    wide_count = lax.axis_size("wide")
    lane_count = lax.axis_size("narrow")
    owner_index = lax.axis_index("wide")
    prompt_lane = lax.axis_index("narrow")
    query_rows = queries[0]
    own_keys = key_rows[0]
    payload_lines = values[0]
    row_count, head_width = own_keys.shape
    tables = pair_tables(head_width, wide_count)
    lead_all, trail_all, doubled_all = (tables[0], tables[1], tables[2])
    padded_rows = tables[4]
    rows_per = padded_rows // wide_count
    position = owner_index * row_count + lax.iota(jnp.int32, row_count)
    live_mask = (position < lengths[0]).astype(jnp.float32)
    cumulative = jnp.cumsum(log_gate[0] * live_mask)
    piece_number = cumulative[-1]
    scaled = live_mask * jnp.exp(piece_number - cumulative)
    spread = (scaled[:, None] * payload_lines.astype(jnp.float32)).astype(jnp.bfloat16)
    span_state = block_state(own_keys, spread, tables)
    totals = lax.all_gather(piece_number[None], "wide", axis=0, tiled=True)
    sent_slices = lax.all_to_all(
        span_state.reshape(wide_count, rows_per, head_width),
        "wide",
        split_axis=0,
        concat_axis=0,
        tiled=True,
    )
    rounded = owner_prefix(sent_slices, totals).astype(jnp.bfloat16)
    carried_slices = lax.all_to_all(
        rounded[:wide_count], "wide", split_axis=0, concat_axis=0, tiled=True
    )
    carried = carried_slices.reshape(padded_rows, head_width)
    final_slice = rounded[wide_count]
    prompt_out = prompt_rows(
        query_rows, own_keys, payload_lines, cumulative, live_mask, carried, tables
    )
    prompt_ids = lax.iota(jnp.int32, lane_count)[:, None]
    chosen = (cont_prompt[None, :] == prompt_ids)[:, :, None]
    masked = jnp.where(chosen, cont_queries[None, :, :], jnp.zeros_like(cont_queries)[None, :, :])
    pair_rows = lax.all_gather(masked, "narrow", axis=1, tiled=True)
    own_rows = lax.dynamic_index_in_dim(pair_rows, prompt_lane, 0, keepdims=False)
    initial = jnp.zeros((own_rows.shape[0], head_width), jnp.float32)
    shard_portion = lax.all_gather(final_slice, "wide", axis=0, tiled=True)
    piece_rows = shard_portion.shape[0]
    features = pair_block(
        own_rows,
        lax.slice_in_dim(lead_all, 0, piece_rows, axis=0),
        lax.slice_in_dim(trail_all, 0, piece_rows, axis=0),
        lax.slice_in_dim(doubled_all, 0, piece_rows, axis=0),
    )
    partial_value = initial + jnp.dot(features, shard_portion, preferred_element_type=jnp.float32)
    running = lax.psum_scatter(partial_value, "narrow", scatter_dimension=0, tiled=True)
    cont_out = rms_rows(running).astype(jnp.bfloat16)
    return (prompt_out[None], cont_out)


def flip(place, bits):
    for bit in (1, 2):
        if bits & bit:
            place = place + bit - 2 * bit * ((place // bit) % 2)
    return place


def triple(rows):
    high = rows.astype(jnp.bfloat16)
    rest = rows - high.astype(jnp.float32)
    middle = rest.astype(jnp.bfloat16)
    low = (rest - middle.astype(jnp.float32)).astype(jnp.bfloat16)
    return high, middle, low


def prefix_sums(rows, upper):
    high, middle, low = triple(rows)
    add = lambda part: jnp.dot(part, upper, preferred_element_type=jnp.float32)
    return add(high) + add(middle) + add(low)


def gather_kernel(
    n,
    lengths_ref,
    prompt_ref,
    query_ref,
    key_ref,
    value_ref,
    gate_ref,
    cont_ref,
    out_ref,
    cont_out_ref,
    kv,
    gates,
    queries,
    cont_own,
    cont_other,
    scale_carried,
    scale_final,
    carried,
    reach_out,
    reach_in,
    gate_send,
    gate_recv,
    col_send,
    x_send,
    kv_recv,
    pair_send,
    pair_recv,
):
    f32, bf16 = jnp.float32, jnp.bfloat16
    me = lax.axis_index("wide")
    lane = lax.axis_index("narrow")
    row, side = me // 2, me % 2
    levels = n // 2
    tok, width = query_ref.shape[1], query_ref.shape[2]
    cont_count = cont_ref.shape[0]
    cont_pad = cont_own.shape[0]
    mesh_id = pl.DeviceIdType.MESH
    peer_x = me + 1 - 2 * side
    sibling = 1 - lane
    order = {2: (1,), 4: (1, 3, 2)}[levels]

    barrier = pltpu.get_barrier_semaphore()
    for step in range(1, n):
        pl.semaphore_signal(
            barrier, inc=1, device_id={"wide": (me + step) % n}, device_id_type=mesh_id
        )
    pl.semaphore_signal(barrier, inc=1, device_id={"narrow": sibling}, device_id_type=mesh_id)

    kv[me] = jnp.concatenate([value_ref[0], key_ref[0]], axis=1)
    gates[me] = gate_ref[...]
    queries[:tok] = jnp.concatenate([jnp.zeros((tok, width), bf16), query_ref[0]], axis=1)
    cont_own[...] = jnp.zeros_like(cont_own)
    cont_own[:cont_count] = jnp.concatenate(
        [jnp.zeros((cont_count, width), bf16), cont_ref[...]], axis=1
    )

    def send(src, dst, send_sem, recv_sem, where):
        return pltpu.make_async_remote_copy(
            src_ref=src,
            dst_ref=dst,
            send_sem=send_sem,
            recv_sem=recv_sem,
            device_id=where,
            device_id_type=mesh_id,
        )

    pl.semaphore_wait(barrier, n)

    gate_copies = []
    for step in range(1, n):
        to = (me + step) % n
        gate_copies.append(
            send(gate_ref, gates.at[me], gate_send.at[step], gate_recv.at[step], {"wide": to})
        )
    kv_copies = []
    for bits in tuple(reversed(sorted(order))):
        to = 2 * flip(row, bits) + side
        kv_copies.append(
            send(kv.at[me], kv.at[me], col_send.at[bits], kv_recv.at[me], {"wide": to})
        )
    kv_copies.append(send(kv.at[me], kv.at[me], x_send.at[0], kv_recv.at[me], {"wide": peer_x}))
    cont_copy = send(
        cont_own, cont_other, pair_send.at[0], pair_recv.at[0], {"narrow": sibling}
    )
    for copy in gate_copies:
        copy.start()
    for copy in kv_copies:
        copy.start()
    cont_copy.start()

    def wait_block(block):
        send(
            kv.at[block], kv.at[block], x_send.at[0], kv_recv.at[block], {"wide": peer_x}
        ).wait_recv()

    def forward(block, bits):
        copy = send(
            kv.at[block], kv.at[block], x_send.at[bits], kv_recv.at[block], {"wide": peer_x}
        )
        copy.start()
        return copy

    length = lengths_ref[0]
    down = lax.broadcasted_iota(jnp.int32, (tok, tok), 0)
    across = lax.broadcasted_iota(jnp.int32, (tok, tok), 1)
    upper = (down <= across).astype(bf16)
    lower = across <= down
    start = me * tok
    live_row = (start + lax.broadcasted_iota(jnp.int32, (1, tok), 1)) < length
    live_col = (start + lax.broadcasted_iota(jnp.int32, (tok, 1), 0)) < length
    gate_row = jnp.where(live_row, gate_ref[...], 0.0)
    total_col = jnp.sum(jnp.where(lower, gate_row, 0.0), axis=1, keepdims=True)
    total_row = prefix_sums(jnp.broadcast_to(gate_row, (8, tok)), upper)[:1]
    contract = (((1,), (1,)), ((), ()))
    own = kv[me]
    scores = lax.dot_general(queries[:tok], own, contract, preferred_element_type=f32)
    decay = jnp.exp(jnp.where(lower & live_row, total_col - total_row, -jnp.inf))
    local = jnp.dot((scores * scores * decay).astype(bf16), own, preferred_element_type=f32)

    for step in range(1, n):
        block = (me + n - step) % n
        send(
            gate_ref, gates.at[block], gate_send.at[step], gate_recv.at[step], {"wide": block}
        ).wait_recv()
    gate_all = jnp.concatenate([gates[u] for u in range(n)], axis=0)
    block_id = lax.broadcasted_iota(jnp.int32, (n, tok), 0)
    live_all = block_id * tok + lax.broadcasted_iota(jnp.int32, (n, tok), 1) < length
    sums = prefix_sums(jnp.where(live_all, gate_all, 0.0), upper)
    ends = sums[:, tok - 1 :]
    rest = ends - sums
    to_me = rest
    to_end = rest
    for v in range(1, n):
        end_v = jnp.where(block_id < v, ends[v : v + 1], 0.0)
        to_end = to_end + end_v
        to_me = to_me + jnp.where(v < me, end_v, 0.0)
    to_me = jnp.exp(jnp.where(live_all & (block_id < me), to_me, -jnp.inf))
    to_end = jnp.exp(jnp.where(live_all, to_end, -jnp.inf))
    for u in range(n):
        scale_carried[u] = to_me[u : u + 1]
        scale_final[u] = to_end[u : u + 1]

    cont_copy.wait()
    queries[tok : tok + cont_pad] = cont_own[...]
    queries[tok + cont_pad :] = cont_other[...]

    cont_scores = lax.dot_general(queries[tok:], own, contract, preferred_element_type=f32)
    cont_weights = (cont_scores * cont_scores * scale_final[me]).astype(bf16)
    carried[:tok] = jnp.zeros((tok, 2 * width), f32)
    carried[tok:] = jnp.dot(cont_weights, own, preferred_element_type=f32)

    def add_block(block):
        lines = kv[block]
        scores = lax.dot_general(queries[...], lines, contract, preferred_element_type=f32)
        scores = scores * scores
        weights = jnp.concatenate(
            [scores[:tok] * scale_carried[block], scores[tok:] * scale_final[block]], axis=0
        ).astype(bf16)
        carried[...] += jnp.dot(weights, lines, preferred_element_type=f32)

    forwards = []
    wait_block(peer_x)
    add_block(peer_x)
    for bits in order:
        block = 2 * flip(row, bits) + side
        wait_block(block)
        forwards.append(forward(block, bits))
        add_block(block)
    for bits in order:
        block = 2 * flip(row, bits) + 1 - side
        wait_block(block)
        add_block(block)

    reach_out[...] = carried[tok + cont_pad :]
    reach_copy = send(
        reach_out, reach_in, pair_send.at[1], pair_recv.at[1], {"narrow": sibling}
    )
    reach_copy.start()

    def rms(rows):
        rows = rows[:, :width]
        square = jnp.sum(rows * rows, axis=1, keepdims=True) * (1.0 / width)
        return rows * lax.rsqrt(square + epsilon)

    result = rms(local + jnp.exp(total_col) * carried[:tok])
    out_ref[0] = jnp.where(live_col, result, 0.0).astype(bf16)

    row_id = lax.broadcasted_iota(jnp.int32, (cont_pad, 2 * width), 0)
    prompts = jnp.zeros((cont_pad, 2 * width), jnp.int32)
    for r in range(cont_count):
        prompts = jnp.where(row_id == r, prompt_ref[r], prompts)
    reach_copy.wait()
    reach = jnp.where(prompts == lane, carried[tok : tok + cont_pad], reach_in[...])
    cont_out_ref[...] = rms(reach)[:cont_count].astype(bf16)

    for copy in gate_copies + kv_copies + forwards:
        copy.wait_send()


def gathered(n, queries, key_rows, values, log_gate, lengths, cont_queries, cont_prompt):
    tok, width = queries.shape[1], queries.shape[2]
    cont_count = cont_queries.shape[0]
    cont_pad = -(-cont_count // 16) * 16
    levels = n // 2
    vmem = pl.BlockSpec(memory_space=pltpu.VMEM)
    smem = pl.BlockSpec(memory_space=pltpu.SMEM)
    dma = lambda count: pltpu.SemaphoreType.DMA((count,))
    f32, bf16 = jnp.float32, jnp.bfloat16
    return pl.pallas_call(
        functools.partial(gather_kernel, n),
        name="retention",
        out_shape=(
            jax.ShapeDtypeStruct((1, tok, width), bf16),
            jax.ShapeDtypeStruct((cont_count, width), bf16),
        ),
        in_specs=[smem, smem, vmem, vmem, vmem, vmem, vmem],
        out_specs=(vmem, vmem),
        scratch_shapes=[
            pltpu.VMEM((n, tok, 2 * width), bf16),
            pltpu.VMEM((n, 1, tok), f32),
            pltpu.VMEM((tok + 2 * cont_pad, 2 * width), bf16),
            pltpu.VMEM((cont_pad, 2 * width), bf16),
            pltpu.VMEM((cont_pad, 2 * width), bf16),
            pltpu.VMEM((n, 1, tok), f32),
            pltpu.VMEM((n, 1, tok), f32),
            pltpu.VMEM((tok + 2 * cont_pad, 2 * width), f32),
            pltpu.VMEM((cont_pad, 2 * width), f32),
            pltpu.VMEM((cont_pad, 2 * width), f32),
            dma(n),
            dma(n),
            dma(levels),
            dma(levels),
            dma(n),
            dma(2),
            dma(2),
        ],
        compiler_params=pltpu.CompilerParams(collective_id=0, has_side_effects=True),
    )(lengths, cont_prompt, queries, key_rows, values, log_gate, cont_queries)


def solution(mesh):
    in_specs = (
        P(("groups", "narrow"), "wide", None),
        P(("groups", "narrow"), "wide", None),
        P(("groups", "narrow"), "wide", None),
        P(("groups", "narrow"), "wide"),
        P(("groups", "narrow")),
        P(("groups", "wide", "narrow"), None),
        P(("groups", "wide", "narrow")),
    )
    out_specs = (P(("groups", "narrow"), "wide", None), P(("groups", "wide", "narrow"), None))
    wide_count = mesh.shape["wide"]
    direct = mesh.shape["narrow"] == 2 and wide_count in (4, 8)
    program = functools.partial(gathered, wide_count) if direct else on_device
    return jax.shard_map(
        program, mesh=mesh, in_specs=in_specs, out_specs=out_specs, check_vma=False
    )
```

```python
import functools

import jax
import jax.numpy as jnp
import numpy as np
from jax import lax
from jax.experimental import pallas as pl
from jax.experimental.pallas import tpu as pltpu
from jax.sharding import PartitionSpec as P

epsilon = 1e-06
block_rows = 1024


def rms_rows(running):
    return running * lax.rsqrt(jnp.mean(running * running, axis=-1, keepdims=True) + epsilon)


def extend_zeros(table, pad_count):
    return np.concatenate([table, np.zeros((pad_count,), table.dtype)])


def pair_tables(head_width, shard_count):
    lead_index, trail_index = np.triu_indices(head_width)
    doubled = np.where(lead_index == trail_index, 1.0, 2.0)
    feature_count = lead_index.shape[0]
    padded_rows = -(-feature_count // shard_count) * shard_count
    block_width = min(block_rows, padded_rows)
    full_length = -(-padded_rows // block_width) * block_width
    pad_count = full_length - lead_index.shape[0]
    lead_index = extend_zeros(lead_index, pad_count).astype(np.int32)
    trail_index = extend_zeros(trail_index, pad_count).astype(np.int32)
    doubled = extend_zeros(doubled, pad_count).astype(np.float32)
    live_pairs = (doubled > 0).astype(np.float32)
    return (
        jnp.asarray(lead_index),
        jnp.asarray(trail_index),
        jnp.asarray(doubled),
        jnp.asarray(live_pairs),
        padded_rows,
        block_width,
        full_length,
    )


def pair_block(rows, lead_part, trail_part, forget_multiplier):
    leading_columns = jnp.take(rows, lead_part, axis=1).astype(jnp.float32)
    right_cols = jnp.take(rows, trail_part, axis=1).astype(jnp.float32)
    return (leading_columns * right_cols * forget_multiplier[None, :]).astype(jnp.bfloat16)


def block_state(key_rows, spread, tables):
    lead_all, trail_all, doubled_all, live_pairs, padded_rows, block_width, full_length = tables
    head_width = key_rows.shape[1]

    def fill_block(block_index, state):
        first_row = block_index * block_width
        features = pair_block(
            key_rows,
            lax.dynamic_slice_in_dim(lead_all, first_row, block_width),
            lax.dynamic_slice_in_dim(trail_all, first_row, block_width),
            lax.dynamic_slice_in_dim(live_pairs, first_row, block_width),
        )
        state_block = lax.dot_general(
            features, spread, (((0,), (0,)), ((), ())), preferred_element_type=jnp.float32
        )
        return lax.dynamic_update_slice_in_dim(
            state, state_block.astype(jnp.bfloat16), first_row, 0
        )

    initial = jnp.zeros((full_length, head_width), jnp.bfloat16)
    return lax.fori_loop(0, full_length // block_width, fill_block, initial)[:padded_rows]


def carried_read(query_rows, carried, tables):
    lead_all, trail_all, doubled_all, live_pairs, padded_rows, block_width, full_length = tables
    row_count, head_width = query_rows.shape
    if full_length > padded_rows:
        carried = jnp.pad(carried, ((0, full_length - padded_rows), (0, 0)))

    def add_block(block_index, running):
        first_row = block_index * block_width
        features = pair_block(
            query_rows,
            lax.dynamic_slice_in_dim(lead_all, first_row, block_width),
            lax.dynamic_slice_in_dim(trail_all, first_row, block_width),
            lax.dynamic_slice_in_dim(doubled_all, first_row, block_width),
        )
        state_rows = lax.dynamic_slice_in_dim(carried, first_row, block_width, 0)
        return running + jnp.dot(features, state_rows, preferred_element_type=jnp.float32)

    return lax.fori_loop(
        0, full_length // block_width, add_block, jnp.zeros((row_count, head_width), jnp.float32)
    )


def owner_prefix(sent_slices, totals):
    shard_count = totals.shape[0]
    inclusive = jnp.cumsum(totals)
    exclusive = jnp.concatenate([jnp.zeros((1,), jnp.float32), inclusive])
    target = lax.iota(jnp.int32, shard_count + 1)[:, None]
    source = lax.iota(jnp.int32, shard_count)[None, :]
    weight = jnp.exp(jnp.where(source < target, exclusive[:, None] - inclusive[None, :], -jnp.inf))
    return jnp.einsum(
        "wu,urn->wrn", weight, sent_slices.astype(jnp.float32), precision=lax.Precision.HIGHEST
    )


def prompt_rows(query_rows, key_rows, payload_lines, cumulative, live_mask, carried, tables):
    row_count, head_width = query_rows.shape
    scores = lax.dot_general(
        query_rows, key_rows, (((1,), (1,)), ((), ())), preferred_element_type=jnp.float32
    )
    row_ids = lax.iota(jnp.int32, row_count)
    lower_mask = row_ids[:, None] >= row_ids[None, :]
    decay_matrix = jnp.exp(
        jnp.where(lower_mask, cumulative[:, None] - cumulative[None, :], -jnp.inf)
    )
    weights = (scores * scores * decay_matrix * live_mask[None, :]).astype(jnp.bfloat16)
    local_term = jnp.dot(weights, payload_lines, preferred_element_type=jnp.float32)
    carried_term = carried_read(query_rows, carried, tables)
    running = local_term + jnp.exp(cumulative)[:, None] * carried_term
    return (live_mask[:, None] * rms_rows(running)).astype(jnp.bfloat16)


def on_device(queries, key_rows, values, log_gate, lengths, cont_queries, cont_prompt):
    wide_count = lax.axis_size("wide")
    lane_count = lax.axis_size("narrow")
    owner_index = lax.axis_index("wide")
    prompt_lane = lax.axis_index("narrow")
    query_rows = queries[0]
    own_keys = key_rows[0]
    payload_lines = values[0]
    row_count, head_width = own_keys.shape
    tables = pair_tables(head_width, wide_count)
    lead_all, trail_all, doubled_all = (tables[0], tables[1], tables[2])
    padded_rows = tables[4]
    rows_per = padded_rows // wide_count
    position = owner_index * row_count + lax.iota(jnp.int32, row_count)
    live_mask = (position < lengths[0]).astype(jnp.float32)
    cumulative = jnp.cumsum(log_gate[0] * live_mask)
    piece_number = cumulative[-1]
    scaled = live_mask * jnp.exp(piece_number - cumulative)
    spread = (scaled[:, None] * payload_lines.astype(jnp.float32)).astype(jnp.bfloat16)
    span_state = block_state(own_keys, spread, tables)
    totals = lax.all_gather(piece_number[None], "wide", axis=0, tiled=True)
    sent_slices = lax.all_to_all(
        span_state.reshape(wide_count, rows_per, head_width),
        "wide",
        split_axis=0,
        concat_axis=0,
        tiled=True,
    )
    rounded = owner_prefix(sent_slices, totals).astype(jnp.bfloat16)
    carried_slices = lax.all_to_all(
        rounded[:wide_count], "wide", split_axis=0, concat_axis=0, tiled=True
    )
    carried = carried_slices.reshape(padded_rows, head_width)
    final_slice = rounded[wide_count]
    prompt_out = prompt_rows(
        query_rows, own_keys, payload_lines, cumulative, live_mask, carried, tables
    )
    prompt_ids = lax.iota(jnp.int32, lane_count)[:, None]
    chosen = (cont_prompt[None, :] == prompt_ids)[:, :, None]
    masked = jnp.where(chosen, cont_queries[None, :, :], jnp.zeros_like(cont_queries)[None, :, :])
    pair_rows = lax.all_gather(masked, "narrow", axis=1, tiled=True)
    own_rows = lax.dynamic_index_in_dim(pair_rows, prompt_lane, 0, keepdims=False)
    initial = jnp.zeros((own_rows.shape[0], head_width), jnp.float32)
    shard_portion = lax.all_gather(final_slice, "wide", axis=0, tiled=True)
    piece_rows = shard_portion.shape[0]
    features = pair_block(
        own_rows,
        lax.slice_in_dim(lead_all, 0, piece_rows, axis=0),
        lax.slice_in_dim(trail_all, 0, piece_rows, axis=0),
        lax.slice_in_dim(doubled_all, 0, piece_rows, axis=0),
    )
    partial_value = initial + jnp.dot(features, shard_portion, preferred_element_type=jnp.float32)
    running = lax.psum_scatter(partial_value, "narrow", scatter_dimension=0, tiled=True)
    cont_out = rms_rows(running).astype(jnp.bfloat16)
    return (prompt_out[None], cont_out)


def flip(place, bits):
    for bit in (1, 2):
        if bits & bit:
            place = place + bit - 2 * bit * ((place // bit) % 2)
    return place


def triple(rows):
    high = rows.astype(jnp.bfloat16)
    rest = rows - high.astype(jnp.float32)
    middle = rest.astype(jnp.bfloat16)
    low = (rest - middle.astype(jnp.float32)).astype(jnp.bfloat16)
    return high, middle, low


def prefix_sums(rows, upper):
    high, middle, low = triple(rows)
    add = lambda part: jnp.dot(part, upper, preferred_element_type=jnp.float32)
    return add(high) + add(middle) + add(low)


def gather_kernel(
    n,
    lengths_ref,
    prompt_ref,
    query_ref,
    key_ref,
    value_ref,
    gate_ref,
    cont_ref,
    out_ref,
    cont_out_ref,
    kv,
    gates,
    queries,
    cont_own,
    cont_other,
    scale_carried,
    scale_final,
    carried,
    reach_out,
    reach_in,
    gate_send,
    gate_recv,
    col_send,
    x_send,
    kv_recv,
    pair_send,
    pair_recv,
):
    f32, bf16 = jnp.float32, jnp.bfloat16
    me = lax.axis_index("wide")
    lane = lax.axis_index("narrow")
    row, side = me // 2, me % 2
    levels = n // 2
    width, tok = query_ref.shape[1], query_ref.shape[2]
    cont_count = cont_ref.shape[0]
    cont_pad = cont_own.shape[0]
    mesh_id = pl.DeviceIdType.MESH
    peer_x = me + 1 - 2 * side
    sibling = 1 - lane
    order = {2: (1,), 4: (1, 3, 2)}[levels]

    barrier = pltpu.get_barrier_semaphore()
    for step in range(1, n):
        pl.semaphore_signal(
            barrier, inc=1, device_id={"wide": (me + step) % n}, device_id_type=mesh_id
        )
    pl.semaphore_signal(barrier, inc=1, device_id={"narrow": sibling}, device_id_type=mesh_id)

    kv[me] = jnp.concatenate([value_ref[0], key_ref[0]], axis=0)
    gates[me] = gate_ref[...]
    queries[:tok] = jnp.transpose(query_ref[0])
    cont_own[...] = jnp.zeros_like(cont_own)
    cont_own[:cont_count, :width] = cont_ref[...]

    def send(src, dst, send_sem, recv_sem, where):
        return pltpu.make_async_remote_copy(
            src_ref=src,
            dst_ref=dst,
            send_sem=send_sem,
            recv_sem=recv_sem,
            device_id=where,
            device_id_type=mesh_id,
        )

    pl.semaphore_wait(barrier, n)

    gate_copies = []
    for step in range(1, n):
        to = (me + step) % n
        gate_copies.append(
            send(gate_ref, gates.at[me], gate_send.at[step], gate_recv.at[step], {"wide": to})
        )
    kv_copies = []
    for bits in tuple(reversed(sorted(order))):
        to = 2 * flip(row, bits) + side
        kv_copies.append(
            send(kv.at[me], kv.at[me], col_send.at[bits], kv_recv.at[me], {"wide": to})
        )
    kv_copies.append(send(kv.at[me], kv.at[me], x_send.at[0], kv_recv.at[me], {"wide": peer_x}))
    cont_copy = send(
        cont_own, cont_other, pair_send.at[0], pair_recv.at[0], {"narrow": sibling}
    )
    for copy in gate_copies:
        copy.start()
    for copy in kv_copies:
        copy.start()
    cont_copy.start()

    def wait_block(block):
        send(
            kv.at[block], kv.at[block], x_send.at[0], kv_recv.at[block], {"wide": peer_x}
        ).wait_recv()

    def forward(block, bits):
        copy = send(
            kv.at[block], kv.at[block], x_send.at[bits], kv_recv.at[block], {"wide": peer_x}
        )
        copy.start()
        return copy

    length = lengths_ref[0]
    down = lax.broadcasted_iota(jnp.int32, (tok, tok), 0)
    across = lax.broadcasted_iota(jnp.int32, (tok, tok), 1)
    upper = (down <= across).astype(bf16)
    lower = across <= down
    start = me * tok
    live_row = (start + lax.broadcasted_iota(jnp.int32, (1, tok), 1)) < length
    gate_row = jnp.where(live_row, gate_ref[...], 0.0)
    total_col = jnp.sum(jnp.where(lower, gate_row, 0.0), axis=1, keepdims=True)
    total_row = prefix_sums(jnp.broadcast_to(gate_row, (8, tok)), upper)[:1]
    contract = (((1,), (1,)), ((), ()))
    scores = jnp.dot(queries[:tok], key_ref[0], preferred_element_type=f32)
    decay = jnp.exp(jnp.where(lower & live_row, total_col - total_row, -jnp.inf))
    local = lax.dot_general(
        (scores * scores * decay).astype(bf16), value_ref[0], contract, preferred_element_type=f32
    )

    for step in range(1, n):
        block = (me + n - step) % n
        send(
            gate_ref, gates.at[block], gate_send.at[step], gate_recv.at[step], {"wide": block}
        ).wait_recv()
    gate_all = jnp.concatenate([gates[u] for u in range(n)], axis=0)
    block_id = lax.broadcasted_iota(jnp.int32, (n, tok), 0)
    live_all = block_id * tok + lax.broadcasted_iota(jnp.int32, (n, tok), 1) < length
    sums = prefix_sums(jnp.where(live_all, gate_all, 0.0), upper)
    ends = sums[:, tok - 1 :]
    rest = ends - sums
    to_me = rest
    to_end = rest
    for v in range(1, n):
        end_v = jnp.where(block_id < v, ends[v : v + 1], 0.0)
        to_end = to_end + end_v
        to_me = to_me + jnp.where(v < me, end_v, 0.0)
    to_me = jnp.exp(jnp.where(live_all & (block_id < me), to_me, -jnp.inf))
    to_end = jnp.exp(jnp.where(live_all, to_end, -jnp.inf))
    for u in range(n):
        scale_carried[u] = to_me[u : u + 1]
        scale_final[u] = to_end[u : u + 1]

    cont_copy.wait()
    queries[tok : tok + cont_pad] = cont_own[:, :width]
    queries[tok + cont_pad :] = cont_other[:, :width]

    cont_scores = jnp.dot(queries[tok:], key_ref[0], preferred_element_type=f32)
    cont_weights = (cont_scores * cont_scores * scale_final[me]).astype(bf16)
    carried[:tok] = jnp.zeros((tok, width), f32)
    carried[tok:] = lax.dot_general(
        cont_weights, value_ref[0], contract, preferred_element_type=f32
    )

    def add_block(block):
        scores = jnp.dot(queries[...], kv[block, width:], preferred_element_type=f32)
        scores = scores * scores
        weights = jnp.concatenate(
            [scores[:tok] * scale_carried[block], scores[tok:] * scale_final[block]], axis=0
        ).astype(bf16)
        carried[...] += lax.dot_general(
            weights, kv[block, :width], contract, preferred_element_type=f32
        )

    forwards = []
    wait_block(peer_x)
    add_block(peer_x)
    for bits in order:
        block = 2 * flip(row, bits) + side
        wait_block(block)
        forwards.append(forward(block, bits))
        add_block(block)
    for bits in order:
        block = 2 * flip(row, bits) + 1 - side
        wait_block(block)
        add_block(block)

    reach_out[:, :width] = carried[tok + cont_pad :]
    reach_copy = send(
        reach_out, reach_in, pair_send.at[1], pair_recv.at[1], {"narrow": sibling}
    )
    reach_copy.start()

    def rms(rows, axis):
        square = jnp.sum(rows * rows, axis=axis, keepdims=True) * (1.0 / width)
        return rows * lax.rsqrt(square + epsilon)

    result = rms(jnp.transpose(local + jnp.exp(total_col) * carried[:tok]), 0)
    out_ref[0] = jnp.where(live_row, result, 0.0).astype(bf16)

    row_id = lax.broadcasted_iota(jnp.int32, (cont_pad, width), 0)
    prompts = jnp.zeros((cont_pad, width), jnp.int32)
    for r in range(cont_count):
        prompts = jnp.where(row_id == r, prompt_ref[r], prompts)
    reach_copy.wait()
    reach = jnp.where(prompts == lane, carried[tok : tok + cont_pad], reach_in[:, :width])
    cont_out_ref[...] = rms(reach, 1)[:cont_count].astype(bf16)

    for copy in gate_copies + kv_copies + forwards:
        copy.wait_send()


def gathered(n, queries, key_rows, values, log_gate, lengths, cont_queries, cont_prompt):
    tok, width = queries.shape[1], queries.shape[2]
    flat = lambda rows: jnp.transpose(rows, (0, 2, 1))
    cont_count = cont_queries.shape[0]
    cont_pad = -(-cont_count // 16) * 16
    levels = n // 2
    vmem = pl.BlockSpec(memory_space=pltpu.VMEM)
    smem = pl.BlockSpec(memory_space=pltpu.SMEM)
    dma = lambda count: pltpu.SemaphoreType.DMA((count,))
    f32, bf16 = jnp.float32, jnp.bfloat16
    prompt_out, cont_out = pl.pallas_call(
        functools.partial(gather_kernel, n),
        name="retention",
        out_shape=(
            jax.ShapeDtypeStruct((1, width, tok), bf16),
            jax.ShapeDtypeStruct((cont_count, width), bf16),
        ),
        in_specs=[smem, smem, vmem, vmem, vmem, vmem, vmem],
        out_specs=(vmem, vmem),
        scratch_shapes=[
            pltpu.VMEM((n, 2 * width, tok), bf16),
            pltpu.VMEM((n, 1, tok), f32),
            pltpu.VMEM((tok + 2 * cont_pad, width), bf16),
            pltpu.VMEM((cont_pad, 2 * width), bf16),
            pltpu.VMEM((cont_pad, 2 * width), bf16),
            pltpu.VMEM((n, 1, tok), f32),
            pltpu.VMEM((n, 1, tok), f32),
            pltpu.VMEM((tok + 2 * cont_pad, width), f32),
            pltpu.VMEM((cont_pad, 2 * width), f32),
            pltpu.VMEM((cont_pad, 2 * width), f32),
            dma(n),
            dma(n),
            dma(levels),
            dma(levels),
            dma(n),
            dma(2),
            dma(2),
        ],
        compiler_params=pltpu.CompilerParams(collective_id=0, has_side_effects=True),
    )(lengths, cont_prompt, flat(queries), flat(key_rows), flat(values), log_gate, cont_queries)
    return flat(prompt_out), cont_out


def solution(mesh):
    in_specs = (
        P(("groups", "narrow"), "wide", None),
        P(("groups", "narrow"), "wide", None),
        P(("groups", "narrow"), "wide", None),
        P(("groups", "narrow"), "wide"),
        P(("groups", "narrow")),
        P(("groups", "wide", "narrow"), None),
        P(("groups", "wide", "narrow")),
    )
    out_specs = (P(("groups", "narrow"), "wide", None), P(("groups", "wide", "narrow"), None))
    wide_count = mesh.shape["wide"]
    direct = mesh.shape["narrow"] == 2 and wide_count in (4, 8)
    program = functools.partial(gathered, wide_count) if direct else on_device
    return jax.shard_map(
        program, mesh=mesh, in_specs=in_specs, out_specs=out_specs, check_vma=False
    )
```

```python
import functools

import jax
import jax.numpy as jnp
import numpy as np
from jax import lax
from jax.experimental import pallas as pl
from jax.experimental.pallas import tpu as pltpu
from jax.sharding import PartitionSpec as P

epsilon = 1e-06
block_rows = 1024


def rms_rows(running):
    return running * lax.rsqrt(jnp.mean(running * running, axis=-1, keepdims=True) + epsilon)


def extend_zeros(table, pad_count):
    return np.concatenate([table, np.zeros((pad_count,), table.dtype)])


def pair_tables(head_width, shard_count):
    lead_index, trail_index = np.triu_indices(head_width)
    doubled = np.where(lead_index == trail_index, 1.0, 2.0)
    feature_count = lead_index.shape[0]
    padded_rows = -(-feature_count // shard_count) * shard_count
    block_width = min(block_rows, padded_rows)
    full_length = -(-padded_rows // block_width) * block_width
    pad_count = full_length - lead_index.shape[0]
    lead_index = extend_zeros(lead_index, pad_count).astype(np.int32)
    trail_index = extend_zeros(trail_index, pad_count).astype(np.int32)
    doubled = extend_zeros(doubled, pad_count).astype(np.float32)
    live_pairs = (doubled > 0).astype(np.float32)
    return (
        jnp.asarray(lead_index),
        jnp.asarray(trail_index),
        jnp.asarray(doubled),
        jnp.asarray(live_pairs),
        padded_rows,
        block_width,
        full_length,
    )


def pair_block(rows, lead_part, trail_part, forget_multiplier):
    leading_columns = jnp.take(rows, lead_part, axis=1).astype(jnp.float32)
    right_cols = jnp.take(rows, trail_part, axis=1).astype(jnp.float32)
    return (leading_columns * right_cols * forget_multiplier[None, :]).astype(jnp.bfloat16)


def block_state(key_rows, spread, tables):
    lead_all, trail_all, doubled_all, live_pairs, padded_rows, block_width, full_length = tables
    head_width = key_rows.shape[1]

    def fill_block(block_index, state):
        first_row = block_index * block_width
        features = pair_block(
            key_rows,
            lax.dynamic_slice_in_dim(lead_all, first_row, block_width),
            lax.dynamic_slice_in_dim(trail_all, first_row, block_width),
            lax.dynamic_slice_in_dim(live_pairs, first_row, block_width),
        )
        state_block = lax.dot_general(
            features, spread, (((0,), (0,)), ((), ())), preferred_element_type=jnp.float32
        )
        return lax.dynamic_update_slice_in_dim(
            state, state_block.astype(jnp.bfloat16), first_row, 0
        )

    initial = jnp.zeros((full_length, head_width), jnp.bfloat16)
    return lax.fori_loop(0, full_length // block_width, fill_block, initial)[:padded_rows]


def carried_read(query_rows, carried, tables):
    lead_all, trail_all, doubled_all, live_pairs, padded_rows, block_width, full_length = tables
    row_count, head_width = query_rows.shape
    if full_length > padded_rows:
        carried = jnp.pad(carried, ((0, full_length - padded_rows), (0, 0)))

    def add_block(block_index, running):
        first_row = block_index * block_width
        features = pair_block(
            query_rows,
            lax.dynamic_slice_in_dim(lead_all, first_row, block_width),
            lax.dynamic_slice_in_dim(trail_all, first_row, block_width),
            lax.dynamic_slice_in_dim(doubled_all, first_row, block_width),
        )
        state_rows = lax.dynamic_slice_in_dim(carried, first_row, block_width, 0)
        return running + jnp.dot(features, state_rows, preferred_element_type=jnp.float32)

    return lax.fori_loop(
        0, full_length // block_width, add_block, jnp.zeros((row_count, head_width), jnp.float32)
    )


def owner_prefix(sent_slices, totals):
    shard_count = totals.shape[0]
    inclusive = jnp.cumsum(totals)
    exclusive = jnp.concatenate([jnp.zeros((1,), jnp.float32), inclusive])
    target = lax.iota(jnp.int32, shard_count + 1)[:, None]
    source = lax.iota(jnp.int32, shard_count)[None, :]
    weight = jnp.exp(jnp.where(source < target, exclusive[:, None] - inclusive[None, :], -jnp.inf))
    return jnp.einsum(
        "wu,urn->wrn", weight, sent_slices.astype(jnp.float32), precision=lax.Precision.HIGHEST
    )


def prompt_rows(query_rows, key_rows, payload_lines, cumulative, live_mask, carried, tables):
    row_count, head_width = query_rows.shape
    scores = lax.dot_general(
        query_rows, key_rows, (((1,), (1,)), ((), ())), preferred_element_type=jnp.float32
    )
    row_ids = lax.iota(jnp.int32, row_count)
    lower_mask = row_ids[:, None] >= row_ids[None, :]
    decay_matrix = jnp.exp(
        jnp.where(lower_mask, cumulative[:, None] - cumulative[None, :], -jnp.inf)
    )
    weights = (scores * scores * decay_matrix * live_mask[None, :]).astype(jnp.bfloat16)
    local_term = jnp.dot(weights, payload_lines, preferred_element_type=jnp.float32)
    carried_term = carried_read(query_rows, carried, tables)
    running = local_term + jnp.exp(cumulative)[:, None] * carried_term
    return (live_mask[:, None] * rms_rows(running)).astype(jnp.bfloat16)


def on_device(queries, key_rows, values, log_gate, lengths, cont_queries, cont_prompt):
    wide_count = lax.axis_size("wide")
    lane_count = lax.axis_size("narrow")
    owner_index = lax.axis_index("wide")
    prompt_lane = lax.axis_index("narrow")
    query_rows = queries[0]
    own_keys = key_rows[0]
    payload_lines = values[0]
    row_count, head_width = own_keys.shape
    tables = pair_tables(head_width, wide_count)
    lead_all, trail_all, doubled_all = (tables[0], tables[1], tables[2])
    padded_rows = tables[4]
    rows_per = padded_rows // wide_count
    position = owner_index * row_count + lax.iota(jnp.int32, row_count)
    live_mask = (position < lengths[0]).astype(jnp.float32)
    cumulative = jnp.cumsum(log_gate[0] * live_mask)
    piece_number = cumulative[-1]
    scaled = live_mask * jnp.exp(piece_number - cumulative)
    spread = (scaled[:, None] * payload_lines.astype(jnp.float32)).astype(jnp.bfloat16)
    span_state = block_state(own_keys, spread, tables)
    totals = lax.all_gather(piece_number[None], "wide", axis=0, tiled=True)
    sent_slices = lax.all_to_all(
        span_state.reshape(wide_count, rows_per, head_width),
        "wide",
        split_axis=0,
        concat_axis=0,
        tiled=True,
    )
    rounded = owner_prefix(sent_slices, totals).astype(jnp.bfloat16)
    carried_slices = lax.all_to_all(
        rounded[:wide_count], "wide", split_axis=0, concat_axis=0, tiled=True
    )
    carried = carried_slices.reshape(padded_rows, head_width)
    final_slice = rounded[wide_count]
    prompt_out = prompt_rows(
        query_rows, own_keys, payload_lines, cumulative, live_mask, carried, tables
    )
    prompt_ids = lax.iota(jnp.int32, lane_count)[:, None]
    chosen = (cont_prompt[None, :] == prompt_ids)[:, :, None]
    masked = jnp.where(chosen, cont_queries[None, :, :], jnp.zeros_like(cont_queries)[None, :, :])
    pair_rows = lax.all_gather(masked, "narrow", axis=1, tiled=True)
    own_rows = lax.dynamic_index_in_dim(pair_rows, prompt_lane, 0, keepdims=False)
    initial = jnp.zeros((own_rows.shape[0], head_width), jnp.float32)
    shard_portion = lax.all_gather(final_slice, "wide", axis=0, tiled=True)
    piece_rows = shard_portion.shape[0]
    features = pair_block(
        own_rows,
        lax.slice_in_dim(lead_all, 0, piece_rows, axis=0),
        lax.slice_in_dim(trail_all, 0, piece_rows, axis=0),
        lax.slice_in_dim(doubled_all, 0, piece_rows, axis=0),
    )
    partial_value = initial + jnp.dot(features, shard_portion, preferred_element_type=jnp.float32)
    running = lax.psum_scatter(partial_value, "narrow", scatter_dimension=0, tiled=True)
    cont_out = rms_rows(running).astype(jnp.bfloat16)
    return (prompt_out[None], cont_out)


def flip(place, bits):
    for bit in (1, 2):
        if bits & bit:
            place = place + bit - 2 * bit * ((place // bit) % 2)
    return place


def triple(rows):
    high = rows.astype(jnp.bfloat16)
    rest = rows - high.astype(jnp.float32)
    middle = rest.astype(jnp.bfloat16)
    low = (rest - middle.astype(jnp.float32)).astype(jnp.bfloat16)
    return high, middle, low


def prefix_sums(rows, upper):
    high, middle, low = triple(rows)
    add = lambda part: jnp.dot(part, upper, preferred_element_type=jnp.float32)
    return add(high) + add(middle) + add(low)


def gather_kernel(
    n,
    lengths_ref,
    prompt_ref,
    query_hbm,
    key_hbm,
    value_hbm,
    gate_ref,
    cont_ref,
    out_ref,
    cont_out_ref,
    query_ref,
    load_sem,
    kv,
    gates,
    queries,
    cont_own,
    cont_other,
    scale_carried,
    scale_final,
    carried,
    reach_out,
    reach_in,
    gate_send,
    gate_recv,
    col_send,
    x_send,
    kv_recv,
    pair_send,
    pair_recv,
):
    f32, bf16 = jnp.float32, jnp.bfloat16
    me = lax.axis_index("wide")
    lane = lax.axis_index("narrow")
    row, side = me // 2, me % 2
    levels = n // 2
    width, tok = query_ref.shape
    cont_count = cont_ref.shape[0]
    cont_pad = cont_own.shape[0]
    mesh_id = pl.DeviceIdType.MESH
    peer_x = me + 1 - 2 * side
    sibling = 1 - lane
    order = {2: (1,), 4: (1, 3, 2)}[levels]

    barrier = pltpu.get_barrier_semaphore()
    for step in range(1, n):
        pl.semaphore_signal(
            barrier, inc=1, device_id={"wide": (me + step) % n}, device_id_type=mesh_id
        )
    pl.semaphore_signal(barrier, inc=1, device_id={"narrow": sibling}, device_id_type=mesh_id)

    loads = [
        pltpu.make_async_copy(value_hbm.at[0], kv.at[me, :width], load_sem.at[0]),
        pltpu.make_async_copy(key_hbm.at[0], kv.at[me, width:], load_sem.at[1]),
        pltpu.make_async_copy(query_hbm.at[0], query_ref, load_sem.at[2]),
    ]
    for load in loads:
        load.start()
    gates[me] = gate_ref[...]
    cont_own[...] = jnp.zeros_like(cont_own)
    cont_own[:cont_count, :width] = cont_ref[...]

    def send(src, dst, send_sem, recv_sem, where):
        return pltpu.make_async_remote_copy(
            src_ref=src,
            dst_ref=dst,
            send_sem=send_sem,
            recv_sem=recv_sem,
            device_id=where,
            device_id_type=mesh_id,
        )

    for load in loads:
        load.wait()
    queries[:tok] = jnp.transpose(query_ref[...])
    pl.semaphore_wait(barrier, n)

    gate_copies = []
    for step in range(1, n):
        to = (me + step) % n
        gate_copies.append(
            send(gate_ref, gates.at[me], gate_send.at[step], gate_recv.at[step], {"wide": to})
        )
    def x_move(block, half, bits):
        lines = kv.at[block, pl.ds(half * width, width)]
        return send(
            lines, lines, x_send.at[bits, half], kv_recv.at[block, half], {"wide": peer_x}
        )

    kv_copies = []
    for bits in tuple(reversed(sorted(order))):
        to = 2 * flip(row, bits) + side
        for half in range(2):
            kv_copies.append(
                send(
                    kv.at[me, pl.ds(half * width, width)],
                    kv.at[me, pl.ds(half * width, width)],
                    col_send.at[bits, half],
                    kv_recv.at[me, half],
                    {"wide": to},
                )
            )
    for half in range(2):
        kv_copies.append(x_move(me, half, 0))
    cont_copy = send(
        cont_own, cont_other, pair_send.at[0], pair_recv.at[0], {"narrow": sibling}
    )
    for copy in gate_copies:
        copy.start()
    for copy in kv_copies:
        copy.start()
    cont_copy.start()

    def wait_block(block):
        for half in range(2):
            x_move(block, half, 0).wait_recv()

    def forward(block, bits, half):
        copy = x_move(block, half, bits)
        copy.wait_recv()
        copy.start()
        return copy

    length = lengths_ref[0]
    down = lax.broadcasted_iota(jnp.int32, (tok, tok), 0)
    across = lax.broadcasted_iota(jnp.int32, (tok, tok), 1)
    upper = (down <= across).astype(bf16)
    lower = across <= down
    start = me * tok
    live_row = (start + lax.broadcasted_iota(jnp.int32, (1, tok), 1)) < length
    gate_row = jnp.where(live_row, gate_ref[...], 0.0)
    total_col = jnp.sum(jnp.where(lower, gate_row, 0.0), axis=1, keepdims=True)
    total_row = prefix_sums(jnp.broadcast_to(gate_row, (8, tok)), upper)[:1]
    contract = (((1,), (1,)), ((), ()))
    scores = jnp.dot(queries[:tok], kv[me, width:], preferred_element_type=f32)
    decay = jnp.exp(jnp.where(lower & live_row, total_col - total_row, -jnp.inf))
    local = lax.dot_general(
        (scores * scores * decay).astype(bf16), kv[me, :width], contract, preferred_element_type=f32
    )

    for step in range(1, n):
        block = (me + n - step) % n
        send(
            gate_ref, gates.at[block], gate_send.at[step], gate_recv.at[step], {"wide": block}
        ).wait_recv()
    gate_all = jnp.concatenate([gates[u] for u in range(n)], axis=0)
    block_id = lax.broadcasted_iota(jnp.int32, (n, tok), 0)
    live_all = block_id * tok + lax.broadcasted_iota(jnp.int32, (n, tok), 1) < length
    sums = prefix_sums(jnp.where(live_all, gate_all, 0.0), upper)
    ends = sums[:, tok - 1 :]
    rest = ends - sums
    to_me = rest
    to_end = rest
    for v in range(1, n):
        end_v = jnp.where(block_id < v, ends[v : v + 1], 0.0)
        to_end = to_end + end_v
        to_me = to_me + jnp.where(v < me, end_v, 0.0)
    to_me = jnp.exp(jnp.where(live_all & (block_id < me), to_me, -jnp.inf))
    to_end = jnp.exp(jnp.where(live_all, to_end, -jnp.inf))
    for u in range(n):
        scale_carried[u] = to_me[u : u + 1]
        scale_final[u] = to_end[u : u + 1]

    cont_copy.wait()
    queries[tok : tok + cont_pad] = cont_own[:, :width]
    queries[tok + cont_pad :] = cont_other[:, :width]

    cont_scores = jnp.dot(queries[tok:], kv[me, width:], preferred_element_type=f32)
    cont_weights = (cont_scores * cont_scores * scale_final[me]).astype(bf16)
    carried[:tok] = jnp.zeros((tok, width), f32)
    carried[tok:] = lax.dot_general(
        cont_weights, kv[me, :width], contract, preferred_element_type=f32
    )

    def add_block(block):
        scores = jnp.dot(queries[...], kv[block, width:], preferred_element_type=f32)
        scores = scores * scores
        weights = jnp.concatenate(
            [scores[:tok] * scale_carried[block], scores[tok:] * scale_final[block]], axis=0
        ).astype(bf16)
        carried[...] += lax.dot_general(
            weights, kv[block, :width], contract, preferred_element_type=f32
        )

    forwards = []
    for bits in order:
        block = 2 * flip(row, bits) + side
        for half in range(2):
            forwards.append(forward(block, bits, half))
        add_block(block)
    wait_block(peer_x)
    add_block(peer_x)
    for bits in order:
        block = 2 * flip(row, bits) + 1 - side
        wait_block(block)
        add_block(block)

    reach_out[:, :width] = carried[tok + cont_pad :]
    reach_copy = send(
        reach_out, reach_in, pair_send.at[1], pair_recv.at[1], {"narrow": sibling}
    )
    reach_copy.start()

    def rms(rows, axis):
        square = jnp.sum(rows * rows, axis=axis, keepdims=True) * (1.0 / width)
        return rows * lax.rsqrt(square + epsilon)

    result = rms(jnp.transpose(local + jnp.exp(total_col) * carried[:tok]), 0)
    out_ref[0] = jnp.where(live_row, result, 0.0).astype(bf16)

    row_id = lax.broadcasted_iota(jnp.int32, (cont_pad, width), 0)
    prompts = jnp.zeros((cont_pad, width), jnp.int32)
    for r in range(cont_count):
        prompts = jnp.where(row_id == r, prompt_ref[r], prompts)
    reach_copy.wait()
    reach = jnp.where(prompts == lane, carried[tok : tok + cont_pad], reach_in[:, :width])
    cont_out_ref[...] = rms(reach, 1)[:cont_count].astype(bf16)

    for copy in gate_copies + kv_copies + forwards:
        copy.wait_send()


def finish_kernel(prompt_ref, cont_ref, prompt_out_ref, cont_out_ref):
    prompt_out_ref[...] = prompt_ref[...]
    cont_out_ref[...] = cont_ref[...]


def gathered(n, queries, key_rows, values, log_gate, lengths, cont_queries, cont_prompt):
    tok, width = queries.shape[1], queries.shape[2]
    flat = lambda rows: jnp.transpose(rows, (0, 2, 1))
    cont_count = cont_queries.shape[0]
    cont_pad = -(-cont_count // 16) * 16
    levels = n // 2
    vmem = pl.BlockSpec(memory_space=pltpu.VMEM)
    hbm = pl.BlockSpec(memory_space=pl.ANY)
    smem = pl.BlockSpec(memory_space=pltpu.SMEM)
    dma = lambda count: pltpu.SemaphoreType.DMA((count,))
    f32, bf16 = jnp.float32, jnp.bfloat16
    prompt_out, cont_out = pl.pallas_call(
        functools.partial(gather_kernel, n),
        name="retention",
        out_shape=(
            jax.ShapeDtypeStruct((1, width, tok), bf16),
            jax.ShapeDtypeStruct((cont_count, width), bf16),
        ),
        in_specs=[smem, smem, hbm, hbm, hbm, vmem, vmem],
        out_specs=(vmem, vmem),
        scratch_shapes=[
            pltpu.VMEM((width, tok), bf16),
            dma(3),
            pltpu.VMEM((n, 2 * width, tok), bf16),
            pltpu.VMEM((n, 1, tok), f32),
            pltpu.VMEM((tok + 2 * cont_pad, width), bf16),
            pltpu.VMEM((cont_pad, 2 * width), bf16),
            pltpu.VMEM((cont_pad, 2 * width), bf16),
            pltpu.VMEM((n, 1, tok), f32),
            pltpu.VMEM((n, 1, tok), f32),
            pltpu.VMEM((tok + 2 * cont_pad, width), f32),
            pltpu.VMEM((cont_pad, 2 * width), f32),
            pltpu.VMEM((cont_pad, 2 * width), f32),
            dma(n),
            dma(n),
            pltpu.SemaphoreType.DMA((levels, 2)),
            pltpu.SemaphoreType.DMA((levels, 2)),
            pltpu.SemaphoreType.DMA((n, 2)),
            dma(2),
            dma(2),
        ],
        compiler_params=pltpu.CompilerParams(collective_id=0, has_side_effects=True),
    )(lengths, cont_prompt, flat(queries), flat(key_rows), flat(values), log_gate, cont_queries)
    prompt_out, cont_out = pl.pallas_call(
        finish_kernel,
        name="finish",
        out_shape=(
            jax.ShapeDtypeStruct(prompt_out.shape, bf16),
            jax.ShapeDtypeStruct(cont_out.shape, bf16),
        ),
        in_specs=[vmem, vmem],
        out_specs=(vmem, vmem),
    )(prompt_out, cont_out)
    return flat(prompt_out), cont_out


def solution(mesh):
    in_specs = (
        P(("groups", "narrow"), "wide", None),
        P(("groups", "narrow"), "wide", None),
        P(("groups", "narrow"), "wide", None),
        P(("groups", "narrow"), "wide"),
        P(("groups", "narrow")),
        P(("groups", "wide", "narrow"), None),
        P(("groups", "wide", "narrow")),
    )
    out_specs = (P(("groups", "narrow"), "wide", None), P(("groups", "wide", "narrow"), None))
    wide_count = mesh.shape["wide"]
    direct = mesh.shape["narrow"] == 2 and wide_count in (4, 8)
    program = functools.partial(gathered, wide_count) if direct else on_device
    return jax.shard_map(
        program, mesh=mesh, in_specs=in_specs, out_specs=out_specs, check_vma=False
    )
```
